256 devices in a mesh: dp: 8 (over y, x_hi), ctx: 32 (over x_lo, z, core).
Axes of the slice: x: 4 (x_hi: 2, x_lo: 2; x = x_hi * 2 + x_lo), y: 4, z: 8, core: 2. Of those that a mesh axis runs over, the one named last changes fastest.
Arguments:
- inputs: bfloat16 [8, 32, 128, 4096], P('dp', 'ctx'), may hold values from -6 to 6
- queries: bfloat16 [8, 32, 128, 1024], P('dp', 'ctx'), may hold values from -6 to 6
- keys_values: bfloat16 [8, 32, 128, 256], P('dp', 'ctx'), may hold values from -6 to 6
- out_grad: bfloat16 [8, 32, 128, 1024], P('dp', 'ctx'), may hold values from -6 to 6
- lengths: int32 [8, 10], P('dp'), may hold values from 1 to 1024, 4096 in all within a row
Outputs:
- grad_q: bfloat16 [8, 32, 128, 1024], P('dp', 'ctx')
- grad_kv: bfloat16 [8, 32, 128, 256], P('dp', 'ctx')
- grad_kv_weight: float32 [4096, 256], P('ctx')
The draws below stay inside these ranges and needn't reach their ends.
All inputs are finite; a program needn't handle non-finite values.
Results may differ from the reference program's by a relative error of at most 0.0052.
Values may be sent and summed in bfloat16 or wider, within the bound.
A program may use at most 64 MiB of HBM per device.

```python
import math
import jax
import jax.numpy as jnp
import numpy as np
from jax import lax

D = 4096
HD = 128
HEADS = 8
TOK_DEV = 128
RESPONSES = 4
PIECES = 10
STRIPES = 32
LEN = 4096
ROWS = 8


def to_stripes_drawn(ordered):
    row_count = ordered.shape[0]
    feature_count = ordered.shape[2]
    return jnp.transpose(ordered.reshape(row_count, TOK_DEV, STRIPES, feature_count), (0, 2, 1, 3))


def draw_queries(key, part):
    draw_key = jax.random.fold_in(key, 11)
    entries = jnp.clip(jax.random.normal(draw_key, (ROWS, LEN, HEADS, HD), jnp.float32), -5.0, 5.0)
    return to_stripes_drawn(entries.reshape(ROWS, LEN, HEADS * HD)).astype(jnp.bfloat16)


def draw_keys_values(key, part):
    draw_key = jax.random.fold_in(key, 12)
    key_draw, value_draw = jax.random.split(draw_key, 2)
    key_part = jnp.clip(jax.random.normal(key_draw, (ROWS, LEN, HD), jnp.float32), -5.0, 5.0)
    value_part = jnp.clip(jax.random.normal(value_draw, (ROWS, LEN, HD), jnp.float32), -5.0, 5.0)
    return to_stripes_drawn(jnp.concatenate([key_part, value_part], axis=2)).astype(jnp.bfloat16)


def spiked(values, stream_key, source, target, shards_of, factor):
    def block_of(position):
        return (jnp.arange(values.shape[position]) // (values.shape[position] // shards_of)).reshape((-1,) + (1,) * (values.ndim - 1 - position))

    first = jax.random.permutation(stream_key, shards_of)[block_of(target)]
    second = (block_of(target) + shards_of // 2) % shards_of
    return jnp.where((block_of(source) == first) | (block_of(source) == second), factor * values, values)


def levels(stream_key, extent, shards, low, high):
    loudness, own = 1.0, jax.random.fold_in(stream_key, 6)
    for axis_at, parts in shards:
        heights = jnp.exp(jax.random.uniform(jax.random.fold_in(own, axis_at), (parts,), jnp.float32, low / len(shards), high / len(shards)))
        loudness = loudness * jnp.repeat(heights, extent[axis_at] // parts).reshape([-1 if axis == axis_at else 1 for axis in range(len(extent))])
    return loudness


def length_profile(amount, total, reach, slope):
    portions = [(1 << 20) // math.isqrt(standing ** slope) + 1 for standing in range(2, amount + 1)]
    rest, counts = total - reach - (amount - 1), [1] * (amount - 1)
    while rest > 0:
        candidates = [i for i in range(amount - 1) if counts[i] < reach]
        whole, budget = sum([portions[i] for i in candidates]), rest
        for i in candidates:
            extra = min(reach - counts[i], max(1, budget * portions[i] // whole), rest)
            counts[i] = counts[i] + extra
            rest = rest - extra
    return np.array([reach] + counts)


def uneven_parts(rng, count, total, limit, lean):
    if count == 2:
        one = jax.random.randint(rng, (), max(1, total - limit), min(limit, total - 1) + 1)
        return jnp.stack([one, total - one])
    tallies = jnp.asarray(length_profile(count, total, limit, lean), jnp.int32)
    pairs = (count - 1) // 2
    source_of, receiver = tallies[1:1 + 2 * pairs:2], tallies[2:2 + 2 * pairs:2]
    slack = jnp.minimum(source_of - 1, limit - receiver)
    passed = jax.random.randint(jax.random.fold_in(rng, 1), (pairs,), 0, 1 << 20) % (slack + 1)
    tallies = tallies.at[1:1 + 2 * pairs:2].set(source_of - passed).at[2:2 + 2 * pairs:2].set(receiver + passed)
    return tallies[jax.random.permutation(jax.random.fold_in(rng, 2), count)]


def gaussian(key, dims, width, limit, cuts=(), kind=jnp.bfloat16):
    values = width * jax.random.normal(key, dims, jnp.float32)
    if cuts:
        values = values * levels(key, dims, cuts, -0.22, 0.18)
    return jnp.clip(values, -limit, limit).astype(kind)


def noise_with(rng, shape, width, reach, shards, heavy, held_as=jnp.bfloat16):
    values = width * jax.random.normal(rng, shape, jnp.float32)
    if shards:
        values = values * levels(rng, shape, shards, -0.22, 0.18)
    return jnp.clip(spiked(values, jax.random.fold_in(rng, 3), *heavy), -reach, reach).astype(held_as)


def setup_inputs(seed: int = 0) -> dict:
    splits = jax.random.split(jax.random.key(seed), 6)
    return {
        "inputs": noise_with(splits[0], (ROWS, STRIPES, TOK_DEV, D), 1.0, 6.0, ((0, 8), (1, 32)), (1, 3, 32, 2.75)),
        "queries": draw_queries(jax.random.fold_in(splits[5], 71), 0),
        "keys_values": draw_keys_values(jax.random.fold_in(splits[5], 71), 0),
        "out_grad": gaussian(splits[3], (ROWS, STRIPES, TOK_DEV, HEADS * HD), 1.0, 6.0, ((0, 8), (1, 32))),
        "lengths": jax.vmap(lambda own: uneven_parts(own, PIECES, LEN, LEN // 4, 1))(jax.random.split(splits[4], ROWS)).reshape((ROWS, PIECES)).astype(jnp.int32),
    }


neg_fill = -1e30


def to_positions(banded):
    row_count, stripe_count, local_count, feature_count = banded.shape
    return jnp.transpose(banded, (0, 2, 1, 3)).reshape(row_count, stripe_count * local_count, feature_count)


def to_stripes(ordered, stripe_count):
    row_count, length_all, feature_count = ordered.shape
    return jnp.transpose(ordered.reshape(row_count, length_all // stripe_count, stripe_count, feature_count), (0, 2, 1, 3))


def piece_of(positions, piece_ends):
    return jnp.sum((positions[:, None] >= piece_ends[None, :]).astype(jnp.int32), axis=1)


def allowed_pairs(query_pos, key_pos, piece_ends):
    per_group = RESPONSES + 1
    query_piece = piece_of(query_pos, piece_ends)
    key_piece = piece_of(key_pos, piece_ends)
    same_group = (query_piece // per_group)[:, None] == (key_piece // per_group)[None, :]
    visible = ((key_piece % per_group) == 0)[None, :] | (query_piece[:, None] == key_piece[None, :])
    return (key_pos[None, :] <= query_pos[:, None]) & same_group & visible


def row_backward(q_row, kv_row, grad_row, length_row):
    positions = jnp.arange(LEN, dtype=jnp.int32)
    piece_ends = jnp.cumsum(length_row, dtype=jnp.int32)
    key_part = kv_row[:, :HD]
    value_part = kv_row[:, HD:]
    score_scale = HD ** -0.5
    block_len = min(LEN, 512)
    block_count = LEN // block_len

    def one_block(key_grads, block_index):
        first_pos = block_index * block_len
        q_block = lax.dynamic_slice_in_dim(q_row, first_pos, block_len, 0).reshape(block_len * HEADS, HD)
        grad_block = lax.dynamic_slice_in_dim(grad_row, first_pos, block_len, 0).reshape(block_len * HEADS, HD)
        query_pos = first_pos + jnp.arange(block_len, dtype=jnp.int32)
        allowed = allowed_pairs(query_pos, positions, piece_ends)
        allowed = jnp.broadcast_to(allowed[:, None, :], (block_len, HEADS, LEN)).reshape(block_len * HEADS, LEN)
        scores = jnp.dot(q_block, key_part.T, preferred_element_type=jnp.float32) * score_scale
        row_max = jnp.max(jnp.where(allowed, scores, neg_fill), axis=1, keepdims=True)
        row_sum = jnp.sum(jnp.where(allowed, jnp.exp(scores - row_max), 0.0), axis=1, keepdims=True)
        log_total = row_max + jnp.log(row_sum)
        soft_probs = jnp.where(allowed, jnp.exp(scores - log_total), 0.0)
        prob_grad = jnp.dot(grad_block, value_part.T, preferred_element_type=jnp.float32)
        row_delta = jnp.sum(soft_probs * prob_grad, axis=1, keepdims=True)
        score_grad = soft_probs * (prob_grad - row_delta)
        low_probs = soft_probs.astype(jnp.bfloat16)
        low_score = score_grad.astype(jnp.bfloat16)
        grad_q = jnp.dot(low_score, key_part, preferred_element_type=jnp.float32) * score_scale
        grad_q = grad_q.astype(jnp.bfloat16).reshape(block_len, HEADS * HD)
        key_term = jnp.dot(low_score.T, q_block, preferred_element_type=jnp.float32) * score_scale
        value_term = jnp.dot(low_probs.T, grad_block, preferred_element_type=jnp.float32)
        return key_grads + jnp.concatenate([key_term, value_term], axis=1), grad_q

    key_grads, grad_blocks = lax.scan(one_block, jnp.zeros((LEN, 2 * HD), jnp.float32), jnp.arange(block_count, dtype=jnp.int32))
    return grad_blocks.reshape(LEN, HEADS * HD), key_grads.astype(jnp.bfloat16)


def reference(inputs, queries, keys_values, out_grad, lengths):
    stripe_count = queries.shape[1]
    input_pos = to_positions(inputs)
    query_rows = to_positions(queries)
    kv_rows = to_positions(keys_values)
    grad_rows = to_positions(out_grad)
    grad_q_list = []
    grad_kv_list = []
    weight_total = jnp.zeros((D, 2 * HD), jnp.float32)
    for row_index in range(ROWS):
        grad_q_row, grad_kv_row = row_backward(query_rows[row_index], kv_rows[row_index], grad_rows[row_index], lengths[row_index])
        grad_q_list.append(grad_q_row)
        grad_kv_list.append(grad_kv_row)
        weight_total = weight_total + jnp.dot(input_pos[row_index].T, grad_kv_row, preferred_element_type=jnp.float32)
    grad_q = to_stripes(jnp.stack(grad_q_list), stripe_count)
    grad_kv = to_stripes(jnp.stack(grad_kv_list), stripe_count)
    return grad_q, grad_kv, weight_total / ROWS
```

```python
import functools
import math

import jax
import jax.numpy as jnp
from jax import lax
from jax.experimental import pallas as pl
from jax.experimental.pallas import tpu as pltpu
from jax.sharding import PartitionSpec as P

HD = 128
HEADS = 8
TOK = 128
STRIPES = 32
NZ = STRIPES // 4
RESPONSES = 4
PIECES = 10
DP = 8
D = 4096
KB = 512
NB = TOK * STRIPES // KB
JB = KB // STRIPES
QI = 32
QR = QI * HEADS
NA = TOK // QI
SCALE = HD ** -0.5
LOG2E = math.log2(math.e)
NEG = -1e30
MESH = pl.DeviceIdType.MESH
BF = jnp.bfloat16
F32 = jnp.float32


def place():
    ctx = lax.axis_index("ctx")
    return ctx // (2 * NZ), (ctx // 2) % NZ, ctx % 2


def index(x, z, c):
    return x * (2 * NZ) + z * 2 + c


def greet(ctx_peers, dp_peers):
    barrier = pltpu.get_barrier_semaphore()
    for peer in ctx_peers:
        pl.semaphore_signal(barrier, inc=1, device_id={"ctx": peer}, device_id_type=MESH)
    for peer in dp_peers:
        pl.semaphore_signal(barrier, inc=1, device_id={"dp": peer}, device_id_type=MESH)
    pl.semaphore_wait(barrier, len(ctx_peers) + len(dp_peers))


def remote(src, dst, send_sem, recv_sem, **device):
    return pltpu.make_async_remote_copy(
        src_ref=src, dst_ref=dst, send_sem=send_sem, recv_sem=recv_sem, device_id=device, device_id_type=MESH
    )


def gather_kernel(kv_ref, x_ref, kvall, xs, own_sem, snd, rcv, xown, xsnd, xrcv):
    x, z, c = place()
    me = index(x, z, c)
    sib, xn, dg = index(x, z, 1 - c), index(1 - x, z, c), index(1 - x, z, 1 - c)
    up, dn = index(x, (z + 1) % NZ, c), index(x, (z + NZ - 1) % NZ, c)
    greet([sib, xn, dg, up, dn], [])
    sends = []

    def send(src, slot, peer):
        copy = remote(src, kvall.at[slot], snd.at[len(sends)], rcv.at[slot], ctx=peer)
        copy.start()
        sends.append(copy)

    def arrive(slot):
        remote(kvall.at[slot], kvall.at[slot], snd.at[0], rcv.at[slot], ctx=sib).wait_recv()

    for peer in (xn, up, dn, sib):
        send(kv_ref, me, peer)
    own = pltpu.make_async_copy(kv_ref, kvall.at[me], own_sem)
    own.start()
    mine = x * 2 + c
    x_copies = []
    for m, (xd, cd) in enumerate(((x, 1 - c), (1 - x, c), (1 - x, 1 - c))):
        for zd in range(NZ):
            cols = pl.ds(pl.multiple_of(index(xd, zd, cd) * HD, HD), HD)
            copy = remote(
                x_ref.at[:, cols],
                xs.at[mine, :, pl.ds(zd * HD, HD)],
                xsnd.at[m, zd],
                xrcv.at[mine, zd],
                ctx=index(xd, z, cd),
            )
            copy.start()
            x_copies.append(copy)
    x_own = []
    for zd in range(NZ):
        cols = pl.ds(pl.multiple_of(index(x, zd, c) * HD, HD), HD)
        copy = pltpu.make_async_copy(x_ref.at[:, cols], xs.at[mine, :, pl.ds(zd * HD, HD)], xown.at[zd])
        copy.start()
        x_own.append(copy)
    other = index(1 - x, z, c)
    arrive(other)
    for peer in (up, dn, sib):
        send(kvall.at[other], other, peer)
    half = NZ // 2
    reach = ((half, half - 1), (half - 1, half))
    for d in range(1, half + 1):
        for side in range(2):
            col = x if side == 0 else 1 - x
            for way in range(2):
                if d > reach[side][way]:
                    continue
                slot = index(col, (z + NZ - d) % NZ if way == 0 else (z + d) % NZ, c)
                arrive(slot)
                if d < reach[side][way]:
                    send(kvall.at[slot], slot, up if way == 0 else dn)
                send(kvall.at[slot], slot, sib)
    for xd in range(2):
        for zd in range(NZ):
            arrive(index(xd, zd, 1 - c))
    own.wait()
    for copy in sends:
        copy.wait_send()
    for copy in x_copies:
        copy.wait_send()
    for copy in x_own:
        copy.wait()
    for m, (xd, cd) in enumerate(((x, 1 - c), (1 - x, c), (1 - x, 1 - c))):
        src = xd * 2 + cd
        for zd in range(NZ):
            ref = xs.at[src, :, pl.ds(zd * HD, HD)]
            remote(ref, ref, xsnd.at[m, zd], xrcv.at[src, zd], ctx=sib).wait_recv()


def gather(kv, x):
    n_sends = 4 + 3 + 4 * (NZ // 2 - 1) * 2 - 2 + 2 * (NZ - 1) + 8
    return pl.pallas_call(
        gather_kernel,
        out_shape=(
            jax.ShapeDtypeStruct((STRIPES, TOK, 2 * HD), BF),
            jax.ShapeDtypeStruct((4, TOK, NZ * HD), BF),
        ),
        in_specs=[pl.BlockSpec(memory_space=pltpu.VMEM), pl.BlockSpec(memory_space=pl.ANY)],
        out_specs=(pl.BlockSpec(memory_space=pltpu.VMEM), pl.BlockSpec(memory_space=pl.ANY)),
        scratch_shapes=[
            pltpu.SemaphoreType.DMA,
            pltpu.SemaphoreType.DMA((n_sends,)),
            pltpu.SemaphoreType.DMA((STRIPES,)),
            pltpu.SemaphoreType.DMA((NZ,)),
            pltpu.SemaphoreType.DMA((3, NZ)),
            pltpu.SemaphoreType.DMA((4, NZ)),
        ],
        compiler_params=pltpu.CompilerParams(collective_id=0, has_side_effects=True, vmem_limit_bytes=40 << 20),
        name="gather_kv",
    )(kv, x)


def dot_t(a, b):
    return lax.dot_general(a, b, (((1,), (1,)), ((), ())), preferred_element_type=F32)


def attention_kernel(len_ref, q_ref, g_ref, kv_ref, gq_ref, dkv_ref, dacc, p_s, pg_s, kt_s, k0_s, mb_s, st_s, gt_s):
    stripe = lax.axis_index("ctx")
    ends = []
    total = jnp.int32(0)
    for k in range(PIECES):
        total = total + len_ref[0, k]
        ends.append(total)
    e0, e4, e5 = ends[0], ends[RESPONSES], ends[RESPONSES + 1]
    row = lax.broadcasted_iota(jnp.int32, (KB, HD), 0)
    k0_s[...] = (row % JB) * STRIPES + row // JB

    def prep(b, carry):
        rows = pl.ds(pl.multiple_of(b * JB, JB), JB)
        kt_s[b] = kv_ref[:, rows, :HD].reshape(KB, HD).T
        dacc[b] = jnp.zeros((KB, 2 * HD), F32)
        return carry

    lax.fori_loop(0, NB, prep, 0)
    c2 = SCALE * LOG2E

    def chunk(a, carry):
        q_rows = pl.ds(pl.multiple_of(a * QI, QI), QI)
        qa = jnp.concatenate([q_ref[q_rows, h * HD : (h + 1) * HD] for h in range(HEADS)], axis=0)
        ga = jnp.concatenate([g_ref[q_rows, h * HD : (h + 1) * HD] for h in range(HEADS)], axis=0)
        lane = lax.broadcasted_iota(jnp.int32, (1, HD), 1)
        pos = (a * QI + lane % QI) * STRIPES + stripe
        first = a * (QI * STRIPES) + stripe
        last = first + (QI - 1) * STRIPES
        start = jnp.zeros((1, HD), jnp.int32)
        start_first = jnp.int32(0)
        for e in ends:
            start = jnp.where(pos >= e, e, start)
            start_first = jnp.where(first >= e, e, start_first)
        prompt_end = jnp.where(pos < e4, e0, e5)
        group_start = jnp.where(pos < e4, 0, e4)

        def needed(b):
            low = b * KB
            high = low + KB - 1
            own = (b >= 2 * a) | (high >= start_first)
            return own | ((first < e4) & (e0 > low)) | ((last >= e4) & (e4 <= high) & (e5 > low))

        st_s[0:1, :] = jnp.full((1, QR), NEG, F32)
        st_s[1:3, :] = jnp.zeros((2, QR), F32)
        gt_s[...] = jnp.zeros((HD, QR), F32)

        def forward(b, carry):
            @pl.when(needed(b))
            def _():
                rows = pl.ds(pl.multiple_of(b * JB, JB), JB)
                key = kv_ref[:, rows, :HD].reshape(KB, HD)
                value = kv_ref[:, rows, HD:].reshape(KB, HD)
                s = dot_t(key, qa)
                pg = dot_t(value, ga)
                pg_s[b] = pg
                k0 = k0_s[...]
                base = b * KB
                mask = (k0 <= pos - base) & (
                    (k0 >= start - base) | ((k0 < prompt_end - base) & (k0 >= group_start - base))
                )
                for half in range(QR // HD):
                    cols = slice(half * HD, (half + 1) * HD)
                    sm = jnp.where(mask, s[:, cols], NEG)
                    m_old = st_s[0:1, cols]
                    m_new = jnp.maximum(m_old, jnp.max(sm, axis=0, keepdims=True))
                    p = jnp.exp2((sm - m_new) * c2)
                    alpha = jnp.exp2((m_old - m_new) * c2)
                    p_s[b, :, cols] = p
                    st_s[0:1, cols] = m_new
                    st_s[1:2, cols] = st_s[1:2, cols] * alpha + jnp.sum(p, axis=0, keepdims=True)
                    st_s[2:3, cols] = st_s[2:3, cols] * alpha + jnp.sum(p * pg[:, cols], axis=0, keepdims=True)
                    mb_s[b, 0:1, cols] = m_new

            return carry

        lax.fori_loop(0, 2 * a + 2, forward, 0)
        m_fin = st_s[0:1, :]
        inv = 1.0 / st_s[1:2, :]
        delta = st_s[2:3, :] * inv

        def backward(b, carry):
            @pl.when(needed(b))
            def _():
                factor = jnp.exp2((mb_s[b, 0:1, :] - m_fin) * c2) * inv
                prob = p_s[b] * factor
                ds = (prob * (pg_s[b] - delta)).astype(BF)
                dacc[b, :, :HD] += jnp.dot(ds, qa, preferred_element_type=F32)
                dacc[b, :, HD:] += jnp.dot(prob.astype(BF), ga, preferred_element_type=F32)
                gt_s[...] += jnp.dot(kt_s[b], ds, preferred_element_type=F32)

            return carry

        lax.fori_loop(0, 2 * a + 2, backward, 0)
        gq = (gt_s[...] * SCALE).T.astype(BF)
        for h in range(HEADS):
            gq_ref[q_rows, h * HD : (h + 1) * HD] = gq[h * QI : (h + 1) * QI]
        return carry

    lax.fori_loop(0, NA, chunk, 0)

    def finish(b, carry):
        rows = pl.ds(pl.multiple_of(b * JB, JB), JB)
        dkv_ref[:, rows, :HD] = (dacc[b, :, :HD] * SCALE).astype(BF).reshape(STRIPES, JB, HD)
        dkv_ref[:, rows, HD:] = dacc[b, :, HD:].astype(BF).reshape(STRIPES, JB, HD)
        return carry

    lax.fori_loop(0, NB, finish, 0)


def attention(lengths, q, g, kvall):
    vmem = pl.BlockSpec(memory_space=pltpu.VMEM)
    return pl.pallas_call(
        attention_kernel,
        out_shape=(
            jax.ShapeDtypeStruct((TOK, HEADS * HD), BF),
            jax.ShapeDtypeStruct((STRIPES, TOK, 2 * HD), BF),
        ),
        in_specs=[pl.BlockSpec(memory_space=pltpu.SMEM), vmem, vmem, vmem],
        out_specs=(vmem, vmem),
        scratch_shapes=[
            pltpu.VMEM((NB, KB, 2 * HD), F32),
            pltpu.VMEM((NB, KB, QR), F32),
            pltpu.VMEM((NB, KB, QR), F32),
            pltpu.VMEM((NB, HD, KB), BF),
            pltpu.VMEM((KB, HD), jnp.int32),
            pltpu.VMEM((NB, 8, QR), F32),
            pltpu.VMEM((8, QR), F32),
            pltpu.VMEM((HD, QR), F32),
        ],
        compiler_params=pltpu.CompilerParams(vmem_limit_bytes=40 << 20),
        name="attention_backward",
    )(lengths, q, g, kvall)


def reduce_kernel(
    dkv, xs_hbm, gkv_ref, w_ref, xs, buf1, sx, buf2, sz, buf3, gs, wt, sw, buf4, w5, buf5,
    xs_sem, s1, r1, s2, r2, s3, r3, s4, r4, s5, r5, s6, r6, s7, r7,
):
    x, z, c = place()
    dp = lax.axis_index("dp")
    mine = x * 2 + c
    sib, xn, dg = index(x, z, 1 - c), index(1 - x, z, c), index(1 - x, z, 1 - c)
    z_peers = [index(x, (z + d) % NZ, c) for d in range(1, NZ)]
    dp_peers = [(dp + d) % DP for d in range(1, DP)]
    load = pltpu.make_async_copy(xs_hbm, xs, xs_sem)
    load.start()
    greet([sib, xn, dg] + z_peers, dp_peers)
    order = sorted(range(NZ), key=lambda d: -min(d, NZ - d))
    targets = [(z + d) % NZ for d in order]
    sends = []
    for col in (1 - x, x):
        for t in targets:
            copy = remote(dkv.at[index(col, t, 1 - c)], buf1.at[col, t], s1.at[col, t], r1.at[col, t], ctx=sib)
            copy.start()
            sends.append(copy)

    def take(ref, recv_sem):
        remote(ref, ref, s1.at[0, 0], recv_sem, ctx=sib).wait_recv()

    for t in targets:
        take(buf1.at[1 - x, t], r1.at[1 - x, t])
        sx[t] = (dkv[index(1 - x, t, c)].astype(F32) + buf1[1 - x, t].astype(F32)).astype(BF)
        copy = remote(sx.at[t], buf2.at[t], s2.at[t], r2.at[t], ctx=xn)
        copy.start()
        sends.append(copy)
    acc = None
    for d, t in zip(order, targets):
        take(buf1.at[x, t], r1.at[x, t])
        take(buf2.at[t], r2.at[t])
        part = dkv[index(x, t, c)].astype(F32) + buf1[x, t].astype(F32) + buf2[t].astype(F32)
        if d == 0:
            acc = part
        else:
            sz[t] = part.astype(BF)
            copy = remote(sz.at[t], buf3.at[z], s3.at[t], r3.at[z], ctx=index(x, t, c))
            copy.start()
            sends.append(copy)
    for t in reversed(targets[:-1]):
        take(buf3.at[t], r3.at[t])
        acc = acc + buf3[t].astype(F32)
    low = acc.astype(BF)
    gs[mine] = low
    for k, peer in enumerate((dg, xn, sib)):
        copy = remote(gs.at[mine], gs.at[mine], s4.at[k], r4.at[mine], ctx=peer)
        copy.start()
        sends.append(copy)
    gkv_ref[...] = low
    load.wait()
    for src in (x * 2 + 1 - c, (1 - x) * 2 + c, (1 - x) * 2 + 1 - c):
        take(gs.at[src], r4.at[src])
    wt[...] = lax.dot_general(
        gs[...].reshape(4 * TOK, 2 * HD),
        xs[...].reshape(4 * TOK, NZ * HD),
        (((0,), (0,)), ((), ())),
        preferred_element_type=F32,
    )
    for d, t in zip(order[:-1], targets[:-1]):
        sw[t] = wt[:, pl.ds(pl.multiple_of(t * HD, HD), HD)].astype(BF)
        copy = remote(sw.at[t], buf4.at[z], s5.at[t], r5.at[z], ctx=index(x, t, c))
        copy.start()
        sends.append(copy)
    total = wt[:, pl.ds(pl.multiple_of(z * HD, HD), HD)]
    for t in reversed(targets[:-1]):
        take(buf4.at[t], r5.at[t])
        total = total + buf4[t].astype(F32)
    rows = HD // DP
    w5[...] = (total.T * (1.0 / DP)).reshape(DP, rows, 2 * HD)
    for peer in dp_peers:
        copy = remote(w5.at[peer], buf5.at[dp], s6.at[peer], r6.at[dp], dp=peer)
        copy.start()
        sends.append(copy)
    part = w5[dp]
    for peer in dp_peers:
        take(buf5.at[peer], r6.at[peer])
        part = part + buf5[peer]
    w_ref[dp] = part
    for peer in dp_peers:
        copy = remote(w_ref.at[dp], w_ref.at[dp], s7.at[peer], r7.at[dp], dp=peer)
        copy.start()
        sends.append(copy)
    for peer in dp_peers:
        take(w_ref.at[peer], r7.at[peer])
    for copy in sends:
        copy.wait_send()


def reduce(dkv, xs):
    vmem = pl.BlockSpec(memory_space=pltpu.VMEM)
    sem = pltpu.SemaphoreType.DMA
    block = (TOK, 2 * HD)
    return pl.pallas_call(
        reduce_kernel,
        out_shape=(
            jax.ShapeDtypeStruct(block, BF),
            jax.ShapeDtypeStruct((DP, HD // DP, 2 * HD), F32),
        ),
        in_specs=[vmem, pl.BlockSpec(memory_space=pl.ANY)],
        out_specs=(vmem, vmem),
        scratch_shapes=[
            pltpu.VMEM((4, TOK, NZ * HD), BF),
            pltpu.VMEM((2, NZ) + block, BF),
            pltpu.VMEM((NZ,) + block, BF),
            pltpu.VMEM((NZ,) + block, BF),
            pltpu.VMEM((NZ,) + block, BF),
            pltpu.VMEM((NZ,) + block, BF),
            pltpu.VMEM((4,) + block, BF),
            pltpu.VMEM((2 * HD, NZ * HD), F32),
            pltpu.VMEM((NZ, 2 * HD, HD), BF),
            pltpu.VMEM((NZ, 2 * HD, HD), BF),
            pltpu.VMEM((DP, HD // DP, 2 * HD), F32),
            pltpu.VMEM((DP, HD // DP, 2 * HD), F32),
            sem,
            sem((2, NZ)), sem((2, NZ)),
            sem((NZ,)), sem((NZ,)),
            sem((NZ,)), sem((NZ,)),
            sem((3,)), sem((4,)),
            sem((NZ,)), sem((NZ,)),
            sem((DP,)), sem((DP,)),
            sem((DP,)), sem((DP,)),
        ],
        compiler_params=pltpu.CompilerParams(collective_id=1, has_side_effects=True, vmem_limit_bytes=40 << 20),
        name="reduce_grads",
    )(dkv, xs)


def on_device(inputs, queries, keys_values, out_grad, lengths):
    kvall, xs = gather(keys_values[0, 0], inputs[0, 0])
    grad_q, dkv = attention(lengths, queries[0, 0], out_grad[0, 0], kvall)
    grad_kv, weight = reduce(dkv, xs)
    return grad_q[None, None], grad_kv[None, None], weight.reshape(HD, 2 * HD)


def solution(mesh):
    return jax.shard_map(
        on_device,
        mesh=mesh,
        in_specs=(
            P("dp", "ctx", None, None),
            P("dp", "ctx", None, None),
            P("dp", "ctx", None, None),
            P("dp", "ctx", None, None),
            P("dp", None),
        ),
        out_specs=(P("dp", "ctx", None, None), P("dp", "ctx", None, None), P("ctx", None)),
        check_vma=False,
    )
```

```python
import functools
import math

import jax
import jax.numpy as jnp
from jax import lax
from jax.experimental import pallas as pl
from jax.experimental.pallas import tpu as pltpu
from jax.sharding import PartitionSpec as P

HD = 128
HEADS = 8
TOK = 128
STRIPES = 32
NZ = STRIPES // 4
RESPONSES = 4
PIECES = 10
DP = 8
D = 4096
QI = 32
QR = QI * HEADS
NA = TOK // QI
HT = TOK // 2
NW = 4
SCALE = HD ** -0.5
LOG2E = math.log2(math.e)
NEG = -1e30
MESH = pl.DeviceIdType.MESH
BF = jnp.bfloat16
F32 = jnp.float32


def place():
    ctx = lax.axis_index("ctx")
    return ctx // (2 * NZ), (ctx // 2) % NZ, ctx % 2


def index(x, z, c):
    return x * (2 * NZ) + z * 2 + c


def greet(ctx_peers, dp_peers):
    barrier = pltpu.get_barrier_semaphore()
    for peer in ctx_peers:
        pl.semaphore_signal(barrier, inc=1, device_id={"ctx": peer}, device_id_type=MESH)
    for peer in dp_peers:
        pl.semaphore_signal(barrier, inc=1, device_id={"dp": peer}, device_id_type=MESH)
    pl.semaphore_wait(barrier, len(ctx_peers) + len(dp_peers))


def remote(src, dst, send_sem, recv_sem, **device):
    return pltpu.make_async_remote_copy(
        src_ref=src, dst_ref=dst, send_sem=send_sem, recv_sem=recv_sem, device_id=device, device_id_type=MESH
    )


def dot_t(a, b):
    return lax.dot_general(a, b, (((1,), (1,)), ((), ())), preferred_element_type=F32)


def t_dot(a, b):
    return lax.dot_general(a, b, (((0,), (0,)), ((), ())), preferred_element_type=F32)


def fused_kernel(
    len_ref, x_ref, q_hbm, kv_hbm, g_hbm, gq_ref, gkv_ref, w_ref,
    q_ref, g_ref, kvall, xs, qa_s, ga_s, k0_s, th_s, st_s, mb_s, p_s, pg_s, dacc, gt_s,
    st1, buf1, sx, buf2, sz, buf3, acc, gs, wt, sw, buf4, wz, sb, buf5, w8,
    in_sem, snd, rcv, xown, xsnd, xrcv, s1, r1, s2, r2, s3, r3, s4, r4, s5, r5, s6, r6, s7, r7,
):
    x, z, c = place()
    dp = lax.axis_index("dp")
    me = index(x, z, c)
    mine = x * 2 + c
    sib, xn, dg = index(x, z, 1 - c), index(1 - x, z, c), index(1 - x, z, 1 - c)
    up, dn = index(x, (z + 1) % NZ, c), index(x, (z + NZ - 1) % NZ, c)
    z_peers = [index(x, (z + d) % NZ, c) for d in range(1, NZ)]
    dp_peers = [(dp + d) % DP for d in range(1, DP)]
    own_kv = pltpu.make_async_copy(kv_hbm, kvall.at[me], in_sem.at[0])
    own_q = pltpu.make_async_copy(q_hbm, q_ref, in_sem.at[1])
    own_g = pltpu.make_async_copy(g_hbm, g_ref, in_sem.at[2])
    for copy in (own_kv, own_q, own_g):
        copy.start()
    greet([sib, xn, dg] + z_peers, dp_peers)
    own_kv.wait()

    def send(slot, peer):
        remote(kvall.at[slot], kvall.at[slot], snd, rcv.at[slot], ctx=peer).start()

    def take(ref, recv_sem):
        remote(ref, ref, snd, recv_sem, ctx=sib).wait_recv()

    def arrive(slot):
        take(kvall.at[slot], rcv.at[slot])

    for peer in (xn, up, dn, sib):
        send(me, peer)
    groups = ((x, 1 - c), (1 - x, c), (1 - x, 1 - c))
    for xd, cd in groups:
        for zd in range(NZ):
            cols = pl.ds(pl.multiple_of(index(xd, zd, cd) * HD, HD), HD)
            dst = xs.at[mine, :, pl.ds(zd * HD, HD)]
            remote(x_ref.at[:, cols], dst, xsnd, xrcv.at[mine], ctx=index(xd, z, cd)).start()
    for zd in range(NZ):
        cols = pl.ds(pl.multiple_of(index(x, zd, c) * HD, HD), HD)
        pltpu.make_async_copy(x_ref.at[:, cols], xs.at[mine, :, pl.ds(zd * HD, HD)], xown).start()

    ends = []
    total_len = jnp.int32(0)
    for k in range(PIECES):
        total_len = total_len + len_ref[0, k]
        ends.append(total_len)
    e0, e4, e5 = ends[0], ends[RESPONSES], ends[RESPONSES + 1]
    shape3 = (4, TOK, HD)
    which = lax.broadcasted_iota(jnp.int32, shape3, 0)
    k0_s[...] = lax.broadcasted_iota(jnp.int32, shape3, 1) * STRIPES + (which // 2) * (2 * NZ) + which % 2
    own_q.wait()
    own_g.wait()
    for a in range(NA):
        q_rows = slice(a * QI, (a + 1) * QI)
        for h in range(HEADS):
            qa_s[a, h * QI : (h + 1) * QI] = q_ref[q_rows, h * HD : (h + 1) * HD]
            ga_s[a, h * QI : (h + 1) * QI] = g_ref[q_rows, h * HD : (h + 1) * HD]
        lane = lax.broadcasted_iota(jnp.int32, (1, HD), 1)
        pos = (a * QI + lane % QI) * STRIPES + me
        start = jnp.zeros((1, HD), jnp.int32)
        for e in ends:
            start = jnp.where(pos >= e, e, start)
        th_s[a, 0:1] = pos
        th_s[a, 1:2] = start
        th_s[a, 2:3] = jnp.where(pos < e4, e0, e5)
        th_s[a, 3:4] = jnp.where(pos < e4, 0, e4)
        st_s[a, 0:1] = jnp.full((1, QR), NEG, F32)
        st_s[a, 1:3] = jnp.zeros((2, QR), F32)
    other = index(1 - x, z, c)
    arrive(other)
    for peer in (up, dn, sib):
        send(other, peer)
    c2 = SCALE * LOG2E
    offsets = [2 * QI * a * (a + 1) for a in range(NA)]

    def keys_of(t, rows, cols):
        pairs = [kvall[pl.ds(2 * t, 2), :rows, cols], kvall[pl.ds(2 * NZ + 2 * t, 2), :rows, cols]]
        return jnp.concatenate(pairs, axis=0).reshape(4 * rows, HD)

    def scores_of(n, carry):
        far = (n + 1) // 2
        t = (z + (1 - n % 2) * far + (n % 2) * (NZ - far)) % NZ
        for xd in range(2):
            arrive(index(xd, t, 1 - c))
        for a in range(NA):
            rows = QI * (a + 1)
            s = dot_t(keys_of(t, rows, slice(0, HD)), qa_s[a])
            pg = dot_t(keys_of(t, rows, slice(HD, 2 * HD)), ga_s[a])
            tile = pl.ds(offsets[a], 4 * rows)
            pg_s[t, tile] = pg
            k0 = k0_s[:, :rows].reshape(4 * rows, HD)
            base = 2 * t
            mask = (k0 <= th_s[a, 0:1] - base) & (
                (k0 >= th_s[a, 1:2] - base) | ((k0 < th_s[a, 2:3] - base) & (k0 >= th_s[a, 3:4] - base))
            )
            for half in range(QR // HD):
                cols = slice(half * HD, (half + 1) * HD)
                sm = jnp.where(mask, s[:, cols], NEG)
                m_old = st_s[a, 0:1, cols]
                m_new = jnp.maximum(m_old, jnp.max(sm, axis=0, keepdims=True))
                p = jnp.exp2((sm - m_new) * c2)
                alpha = jnp.exp2((m_old - m_new) * c2)
                p_s[t, tile, cols] = p
                st_s[a, 0:1, cols] = m_new
                st_s[a, 1:2, cols] = st_s[a, 1:2, cols] * alpha + jnp.sum(p, axis=0, keepdims=True)
                st_s[a, 2:3, cols] = st_s[a, 2:3, cols] * alpha + jnp.sum(p * pg[:, cols], axis=0, keepdims=True)
                mb_s[t, a : a + 1, cols] = m_new
        return carry

    half_z = NZ // 2

    def travel(d, carry):
        below, above = (z + NZ - d) % NZ, (z + d) % NZ
        for way, side in ((0, 0), (1, 0), (0, 1), (1, 1)):
            slot = index(x if side == 0 else 1 - x, below if way == 0 else above, c)
            ahead = up if way == 0 else dn
            reach = half_z if way == side else half_z - 1

            @pl.when(d <= reach)
            def _():
                arrive(slot)

            @pl.when(d < reach)
            def _():
                send(slot, ahead)

            @pl.when(d <= reach)
            def _():
                send(slot, sib)

        lax.fori_loop(jnp.maximum(2 * d - 3, 0), jnp.minimum(2 * d - 1, NZ), scores_of, 0)
        return carry

    lax.fori_loop(1, half_z + 2, travel, 0)

    lane2 = lax.broadcasted_iota(jnp.int32, (1, 2 * HD), 1)
    scale_row = jnp.where(lane2 < HD, SCALE, 1.0).astype(F32)

    def plane_at(k):
        return (z + half_z + (1 - 2 * (k % 2)) * ((k + 1) // 2)) % NZ

    def final_rows(slot, a):
        return dacc[slot, a * QI : (a + 1) * QI] * scale_row

    def to_x(a, t):
        take(buf1.at[a, t], r1.at[a, t])
        sx[a, t] = (final_rows(index(1 - x, t, c), a) + buf1[a, t, 1 - x].astype(F32)).astype(BF)
        remote(sx.at[a, t], buf2.at[a, t], s2, r2.at[a, t], ctx=xn).start()

    def to_z(a, k, t):
        take(buf2.at[a, t], r2.at[a, t])
        val = final_rows(index(x, t, c), a) + buf1[a, t, x].astype(F32) + buf2[a, t].astype(F32)

        @pl.when(k < NZ - 1)
        def _():
            sz[a, k] = val.astype(BF)
            remote(sz.at[a, k], buf3.at[a, z], s3, r3.at[a, z], ctx=index(x, t, c)).start()

        @pl.when(k == NZ - 1)
        def _():
            acc[a] = val

    for a in reversed(range(NA)):
        rows = QI * (a + 1)
        tile = pl.ds(offsets[a], 4 * rows)
        gt_s[...] = jnp.zeros((HD, QR), F32)

        def step(k, carry, a=a, rows=rows, tile=tile):
            t = plane_at(k)
            inv = 1.0 / st_s[a, 1:2]
            delta = st_s[a, 2:3] * inv
            factor = jnp.exp2((mb_s[t, a : a + 1] - st_s[a, 0:1]) * c2) * inv
            prob = p_s[t, tile] * factor
            ds = (prob * (pg_s[t, tile] - delta)).astype(BF)
            dk = jnp.dot(ds, qa_s[a], preferred_element_type=F32).reshape(4, rows, HD)
            dv = jnp.dot(prob.astype(BF), ga_s[a], preferred_element_type=F32).reshape(4, rows, HD)
            for xd in range(2):
                slots = pl.ds(2 * NZ * xd + 2 * t, 2)
                if a == NA - 1:
                    dacc[slots, :rows, :HD] = dk[2 * xd : 2 * xd + 2]
                    dacc[slots, :rows, HD:] = dv[2 * xd : 2 * xd + 2]
                else:
                    dacc[slots, :rows, :HD] += dk[2 * xd : 2 * xd + 2]
                    dacc[slots, :rows, HD:] += dv[2 * xd : 2 * xd + 2]
            gt_s[...] += t_dot(keys_of(t, rows, slice(0, HD)), ds)
            for xd in range(2):
                st1[a, t, xd] = final_rows(index(xd, t, 1 - c), a).astype(BF)
            remote(st1.at[a, t], buf1.at[a, t], s1, r1.at[a, t], ctx=sib).start()
            if a + 1 < NA:
                to_x(a + 1, t)
            if a + 2 < NA:
                to_z(a + 2, k, t)
            return carry

        lax.fori_loop(0, NZ, step, 0)
        gq = (gt_s[...] * SCALE).T.astype(BF)
        for h in range(HEADS):
            gq_ref[a * QI : (a + 1) * QI, h * HD : (h + 1) * HD] = gq[h * QI : (h + 1) * QI]

    def tail(k, carry):
        to_x(0, plane_at(k))
        to_z(1, k, plane_at(k))
        return carry

    lax.fori_loop(0, NZ, tail, 0)

    def settle(a):
        val = acc[a]
        for d in (1, NZ - 1, 2, NZ - 2, 3, NZ - 3, half_z):
            t = (z + d) % NZ
            take(buf3.at[a, t], r3.at[a, t])
            val = val + buf3[a, t].astype(F32)
        piece = slice(a * QI, (a + 1) * QI)
        gs[mine, piece] = val.astype(BF)
        gkv_ref[piece] = val.astype(BF)
        for peer in (dg, xn, sib):
            ref = gs.at[mine, piece]
            remote(ref, ref, s4, r4.at[mine], ctx=peer).start()

    settle(3)
    settle(2)

    def last(k, carry):
        to_z(0, k, plane_at(k))
        return carry

    lax.fori_loop(0, NZ, last, 0)
    settle(1)
    settle(0)
    pltpu.make_async_copy(xs.at[mine], xs.at[mine], xown).wait()
    for xd, cd in groups:
        take(xs.at[xd * 2 + cd], xrcv.at[xd * 2 + cd])
    for xd, cd in groups:
        take(gs.at[xd * 2 + cd], r4.at[xd * 2 + cd])
    sends = []
    group = gs[...].reshape(4 * TOK, 2 * HD)
    rows = 2 * HD // DP
    wide = NZ * HD // NW
    for k in range(NW):
        cols = slice(k * wide, (k + 1) * wide)
        wt[:, cols] = lax.dot_general(
            group,
            xs[:, :, cols].reshape(4 * TOK, wide),
            (((0,), (0,)), ((), ())),
            preferred_element_type=F32,
        )
        sw[:, :, cols] = wt[:, cols].astype(BF).reshape(DP, rows, wide)
        for peer in dp_peers:
            copy = remote(
                sw.at[peer, :, cols], buf4.at[dp, :, cols], s5.at[peer, k], r5.at[dp, k], dp=peer
            )
            copy.start()
            sends.append(copy)
    own_rows = pl.ds(pl.multiple_of(dp * rows, rows), rows)
    for k in range(NW):
        cols = slice(k * wide, (k + 1) * wide)
        part = wt[own_rows, cols]
        for peer in dp_peers:
            take(buf4.at[peer, :, cols], r5.at[peer, k])
            part = part + buf4[peer, :, cols].astype(F32)
        for n in range(wide // HD):
            wz[k * (wide // HD) + n] = part[:, n * HD : (n + 1) * HD]
    targets = [(z + d) % NZ for d in (half_z, 3, NZ - 3, 2, NZ - 2, 1, NZ - 1)]
    for t in targets:
        sb[t] = wz[t].astype(BF)
        copy = remote(sb.at[t], buf5.at[z], s6.at[t], r6.at[z], ctx=index(x, t, c))
        copy.start()
        sends.append(copy)
    total = wz[z]
    for t in reversed(targets):
        take(buf5.at[t], r6.at[t])
        total = total + buf5[t].astype(F32)
    w8[dp] = total * (1.0 / DP)
    for peer in dp_peers:
        copy = remote(w8.at[dp], w8.at[dp], s7.at[peer], r7.at[dp], dp=peer)
        copy.start()
        sends.append(copy)
    for peer in dp_peers:
        take(w8.at[peer], r7.at[peer])
    w_ref[...] = w8[...].reshape(2 * HD, HD).T
    for copy in sends:
        copy.wait_send()

    def sent(ref, sem):
        remote(ref, ref, sem, r1.at[0, 0], ctx=sib).wait_send()

    sent(kvall.at[pl.ds(0, 4 + 3 + 10 + 14)], snd)
    sent(xs.at[pl.ds(0, 3)], xsnd)
    sent(st1, s1)
    sent(sx, s2)
    sent(sz, s3)
    sent(gs.at[pl.ds(0, 3)], s4)


def on_device(inputs, queries, keys_values, out_grad, lengths):
    vmem = pl.BlockSpec(memory_space=pltpu.VMEM)
    hbm = pl.BlockSpec(memory_space=pl.ANY)
    sem = pltpu.SemaphoreType.DMA
    tri = 2 * QI * NA * (NA + 1)
    rows = 2 * HD // DP
    piece = (QI, 2 * HD)
    grad_q, grad_kv, weight = pl.pallas_call(
        fused_kernel,
        out_shape=(
            jax.ShapeDtypeStruct((TOK, HEADS * HD), BF),
            jax.ShapeDtypeStruct((TOK, 2 * HD), BF),
            jax.ShapeDtypeStruct((HD, 2 * HD), F32),
        ),
        in_specs=[pl.BlockSpec(memory_space=pltpu.SMEM), hbm, hbm, hbm, hbm],
        out_specs=(vmem, vmem, vmem),
        scratch_shapes=[
            pltpu.VMEM((TOK, HEADS * HD), BF),
            pltpu.VMEM((TOK, HEADS * HD), BF),
            pltpu.VMEM((STRIPES, TOK, 2 * HD), BF),
            pltpu.VMEM((4, TOK, NZ * HD), BF),
            pltpu.VMEM((NA, QR, HD), BF),
            pltpu.VMEM((NA, QR, HD), BF),
            pltpu.VMEM((4, TOK, HD), jnp.int32),
            pltpu.VMEM((NA, 8, HD), jnp.int32),
            pltpu.VMEM((NA, 8, QR), F32),
            pltpu.VMEM((NZ, 8, QR), F32),
            pltpu.VMEM((NZ, tri, QR), F32),
            pltpu.VMEM((NZ, tri, QR), F32),
            pltpu.VMEM((STRIPES, TOK, 2 * HD), F32),
            pltpu.VMEM((HD, QR), F32),
            pltpu.VMEM((NA, NZ, 2) + piece, BF),
            pltpu.VMEM((NA, NZ, 2) + piece, BF),
            pltpu.VMEM((NA, NZ) + piece, BF),
            pltpu.VMEM((NA, NZ) + piece, BF),
            pltpu.VMEM((NA, NZ - 1) + piece, BF),
            pltpu.VMEM((NA, NZ) + piece, BF),
            pltpu.VMEM((NA,) + piece, F32),
            pltpu.VMEM((4, TOK, 2 * HD), BF),
            pltpu.VMEM((2 * HD, NZ * HD), F32),
            pltpu.VMEM((DP, rows, NZ * HD), BF),
            pltpu.VMEM((DP, rows, NZ * HD), BF),
            pltpu.VMEM((NZ, rows, HD), F32),
            pltpu.VMEM((NZ, rows, HD), BF),
            pltpu.VMEM((NZ, rows, HD), BF),
            pltpu.VMEM((DP, rows, HD), F32),
            sem((3,)),
            sem, sem((STRIPES,)),
            sem, sem, sem((4,)),
            sem, sem((NA, NZ)),
            sem, sem((NA, NZ)),
            sem, sem((NA, NZ)),
            sem, sem((4,)),
            sem((DP, NW)), sem((DP, NW)),
            sem((NZ,)), sem((NZ,)),
            sem((DP,)), sem((DP,)),
        ],
        compiler_params=pltpu.CompilerParams(collective_id=0, has_side_effects=True, vmem_limit_bytes=56 << 20),
        name="fused_backward",
    )(lengths, inputs[0, 0], queries[0, 0], keys_values[0, 0], out_grad[0, 0])
    return grad_q[None, None], grad_kv[None, None], weight


def solution(mesh):
    return jax.shard_map(
        on_device,
        mesh=mesh,
        in_specs=(
            P("dp", "ctx", None, None),
            P("dp", "ctx", None, None),
            P("dp", "ctx", None, None),
            P("dp", "ctx", None, None),
            P("dp", None),
        ),
        out_specs=(P("dp", "ctx", None, None), P("dp", "ctx", None, None), P("ctx", None)),
        check_vma=False,
    )
```

```python
import functools
import math

import jax
import jax.numpy as jnp
from jax import lax
from jax.experimental import pallas as pl
from jax.experimental.pallas import tpu as pltpu
from jax.sharding import PartitionSpec as P

HD = 128
HEADS = 8
TOK = 128
STRIPES = 32
NZ = STRIPES // 4
RESPONSES = 4
PIECES = 10
DP = 8
D = 4096
QI = 32
QH = QI * HEADS
QR = 2 * QH
NA = TOK // QI
HT = TOK // 2
NW = 4
SCALE = HD ** -0.5
LOG2E = math.log2(math.e)
NEG = -1e30
MESH = pl.DeviceIdType.MESH
BF = jnp.bfloat16
F32 = jnp.float32


def place():
    ctx = lax.axis_index("ctx")
    return ctx // (2 * NZ), (ctx // 2) % NZ, ctx % 2


def index(x, z, c):
    return x * (2 * NZ) + z * 2 + c


def greet(ctx_peers, dp_peers):
    barrier = pltpu.get_barrier_semaphore()
    for peer in ctx_peers:
        pl.semaphore_signal(barrier, inc=1, device_id={"ctx": peer}, device_id_type=MESH)
    for peer in dp_peers:
        pl.semaphore_signal(barrier, inc=1, device_id={"dp": peer}, device_id_type=MESH)
    pl.semaphore_wait(barrier, len(ctx_peers) + len(dp_peers))


def remote(src, dst, send_sem, recv_sem, **device):
    return pltpu.make_async_remote_copy(
        src_ref=src, dst_ref=dst, send_sem=send_sem, recv_sem=recv_sem, device_id=device, device_id_type=MESH
    )


def dot_t(a, b):
    return lax.dot_general(a, b, (((1,), (1,)), ((), ())), preferred_element_type=F32)


def t_dot(a, b):
    return lax.dot_general(a, b, (((0,), (0,)), ((), ())), preferred_element_type=F32)


def fused_kernel(
    len_ref, x_ref, q_hbm, kv_hbm, g_hbm, gq_ref, gkv_ref, w_ref,
    q_ref, g_ref, q2_ref, g2_ref, kvall, xs, qa_s, ga_s, k0_s, th_s, st_s, st2, mb_s, p_s, pg_s, dacc, gt_s, gq_mine, gq_buf,
    sx, buf2, sz, buf3, acc, gs, wt, sw, buf4, wz, sb, buf5, w8,
    in_sem, snd, rcv, xown, xsnd, xrcv, qsnd, qrcv, s1, r1, gsnd, grcv, s2, r2, s3, r3, s4, r4, s5, r5, s6, r6, s7, r7,
):
    x, z, c = place()
    dp = lax.axis_index("dp")
    me = index(x, z, c)
    mine = x * 2 + c
    sib, xn, dg = index(x, z, 1 - c), index(1 - x, z, c), index(1 - x, z, 1 - c)
    up, dn = index(x, (z + 1) % NZ, c), index(x, (z + NZ - 1) % NZ, c)
    z_peers = [index(x, (z + d) % NZ, c) for d in range(1, NZ)]
    dp_peers = [(dp + d) % DP for d in range(1, DP)]
    own_kv = pltpu.make_async_copy(kv_hbm, kvall.at[me], in_sem.at[0])
    own_q = pltpu.make_async_copy(q_hbm, q_ref, in_sem.at[1])
    own_g = pltpu.make_async_copy(g_hbm, g_ref, in_sem.at[2])
    for copy in (own_kv, own_q, own_g):
        copy.start()
    greet([sib, xn, dg] + z_peers, dp_peers)
    own_kv.wait()

    def send(slot, h, peer):
        ref = kvall.at[slot, pl.ds(h * HT, HT)]
        remote(ref, ref, snd, rcv.at[slot, h], ctx=peer).start()

    def take(ref, recv_sem):
        remote(ref, ref, snd, recv_sem, ctx=sib).wait_recv()

    def arrive(slot, h):
        take(kvall.at[slot, pl.ds(h * HT, HT)], rcv.at[slot, h])

    for h in range(2):
        for peer in (xn, up, dn):
            send(me, h, peer)
    remote(q_hbm, q2_ref, qsnd.at[0], qrcv.at[0], ctx=sib).start()
    remote(g_hbm, g2_ref, qsnd.at[1], qrcv.at[1], ctx=sib).start()
    groups = ((x, 1 - c), (1 - x, c), (1 - x, 1 - c))
    for xd, cd in groups:
        for zd in range(NZ):
            cols = pl.ds(pl.multiple_of(index(xd, zd, cd) * HD, HD), HD)
            dst = xs.at[mine, :, pl.ds(zd * HD, HD)]
            remote(x_ref.at[:, cols], dst, xsnd, xrcv.at[mine], ctx=index(xd, z, cd)).start()
    for zd in range(NZ):
        cols = pl.ds(pl.multiple_of(index(x, zd, c) * HD, HD), HD)
        pltpu.make_async_copy(x_ref.at[:, cols], xs.at[mine, :, pl.ds(zd * HD, HD)], xown).start()

    ends = []
    total_len = jnp.int32(0)
    for k in range(PIECES):
        total_len = total_len + len_ref[0, k]
        ends.append(total_len)
    e0, e4, e5 = ends[0], ends[RESPONSES], ends[RESPONSES + 1]
    shape3 = (2, TOK, HD)
    which = lax.broadcasted_iota(jnp.int32, shape3, 0)
    k0_s[...] = lax.broadcasted_iota(jnp.int32, shape3, 1) * STRIPES + which * (2 * NZ)
    for a in range(NA):
        lane = lax.broadcasted_iota(jnp.int32, (1, QR), 1)
        pos = (a * QI + lane % QI) * STRIPES + index(x, z, 0) + lane // QH
        start = jnp.zeros((1, QR), jnp.int32)
        for e in ends:
            start = jnp.where(pos >= e, e, start)
        th_s[a, 0:1] = pos
        th_s[a, 1:2] = start
        th_s[a, 2:3] = jnp.where(pos < e4, e0, e5)
        th_s[a, 3:4] = jnp.where(pos < e4, 0, e4)
        st_s[a, 0:1] = jnp.full((1, QR), NEG, F32)
        st_s[a, 1:8] = jnp.zeros((7, QR), F32)
    other = index(1 - x, z, c)
    for h in range(2):
        arrive(other, h)
        for peer in (up, dn):
            send(other, h, peer)
    own_q.wait()
    own_g.wait()
    take(q2_ref, qrcv.at[0])
    take(g2_ref, qrcv.at[1])
    for core, q_in, g_in in ((c, q_ref, g_ref), (1 - c, q2_ref, g2_ref)):
        for a in range(NA):
            q_rows = slice(a * QI, (a + 1) * QI)
            for h in range(HEADS):
                to = pl.ds(pl.multiple_of(core * QH + h * QI, QI), QI)
                qa_s[a, to] = q_in[q_rows, h * HD : (h + 1) * HD]
                ga_s[a, to] = g_in[q_rows, h * HD : (h + 1) * HD]
    c2 = SCALE * LOG2E
    offsets = [QI * a * (a + 1) for a in range(NA)]

    def keys_of(t, rows, cols):
        pair = [kvall[pl.ds(index(xd, t, c), 1), :rows, cols] for xd in range(2)]
        return jnp.concatenate(pair, axis=0).reshape(2 * rows, HD)

    def scores_of(n, carry):
        far = (n + 1) // 2
        t = (z + (1 - n % 2) * far + (n % 2) * (NZ - far)) % NZ
        base = 2 * t + c
        for a in range(NA):
            rows = QI * (a + 1)
            s = dot_t(keys_of(t, rows, slice(0, HD)), qa_s[a])
            pg = dot_t(keys_of(t, rows, slice(HD, 2 * HD)), ga_s[a])
            tile = pl.ds(offsets[a], 2 * rows)
            pg_s[t, tile] = pg
            k0 = k0_s[:, :rows].reshape(2 * rows, HD)
            for core in range(2):
                at = slice(core * QH, core * QH + HD)
                mask = (k0 <= th_s[a, 0:1, at] - base) & (
                    (k0 >= th_s[a, 1:2, at] - base)
                    | ((k0 < th_s[a, 2:3, at] - base) & (k0 >= th_s[a, 3:4, at] - base))
                )
                for half in range(QH // HD):
                    cols = slice(core * QH + half * HD, core * QH + (half + 1) * HD)
                    sm = jnp.where(mask, s[:, cols], NEG)
                    m_old = st_s[a, 0:1, cols]
                    m_new = jnp.maximum(m_old, jnp.max(sm, axis=0, keepdims=True))
                    p = jnp.exp2((sm - m_new) * c2)
                    alpha = jnp.exp2((m_old - m_new) * c2)
                    p_s[t, tile, cols] = p
                    st_s[a, 0:1, cols] = m_new
                    st_s[a, 1:2, cols] = st_s[a, 1:2, cols] * alpha + jnp.sum(p, axis=0, keepdims=True)
                    st_s[a, 2:3, cols] = st_s[a, 2:3, cols] * alpha + jnp.sum(p * pg[:, cols], axis=0, keepdims=True)
                    mb_s[t, a : a + 1, cols] = m_new
        return carry

    half_z = NZ // 2

    def travel(d, carry):
        below, above = (z + NZ - d) % NZ, (z + d) % NZ
        for side in range(2):
            for h in range(2):
                for way in range(2):
                    slot = index(x if side == 0 else 1 - x, below if way == 0 else above, c)
                    reach = half_z if way == side else half_z - 1

                    @pl.when((d > 0) & (d <= reach))
                    def _():
                        arrive(slot, h)

                    @pl.when((d > 0) & (d < reach))
                    def _():
                        send(slot, h, up if way == 0 else dn)

        lax.fori_loop(jnp.maximum(2 * d - 1, 0), jnp.minimum(2 * d + 1, NZ), scores_of, 0)
        return carry

    lax.fori_loop(0, half_z + 1, travel, 0)
    remote(st_s, st2, s1, r1, ctx=sib).start()
    take(st2, r1)
    remote(st_s, st_s, s1, r1, ctx=sib).wait_send()
    for a in range(NA):
        m_fin = jnp.maximum(st_s[a, 0:1], st2[a, 0:1])
        low, high = jnp.exp2((st_s[a, 0:1] - m_fin) * c2), jnp.exp2((st2[a, 0:1] - m_fin) * c2)
        inv = 1.0 / (st_s[a, 1:2] * low + st2[a, 1:2] * high)
        delta = (st_s[a, 2:3] * low + st2[a, 2:3] * high) * inv
        st_s[a, 0:1] = m_fin
        st_s[a, 1:2] = inv
        st_s[a, 2:3] = delta

    lane2 = lax.broadcasted_iota(jnp.int32, (1, 2 * HD), 1)
    scale_row = jnp.where(lane2 < HD, SCALE, 1.0).astype(F32)

    def plane_at(k):
        return (z + half_z + (1 - 2 * (k % 2)) * ((k + 1) // 2)) % NZ

    def final_rows(slot, a):
        return dacc[slot, a * QI : (a + 1) * QI] * scale_row

    def to_x(a, t):
        sx[a, t] = final_rows(index(1 - x, t, c), a).astype(BF)
        remote(sx.at[a, t], buf2.at[a, t], s2, r2.at[a, t], ctx=xn).start()

    def to_z(a, k, t):
        take(buf2.at[a, t], r2.at[a, t])
        val = final_rows(index(x, t, c), a) + buf2[a, t].astype(F32)

        @pl.when(k < NZ - 1)
        def _():
            sz[a, k] = val.astype(BF)
            remote(sz.at[a, k], buf3.at[a, z], s3, r3.at[a, z], ctx=index(x, t, c)).start()

        @pl.when(k == NZ - 1)
        def _():
            acc[a] = val

    own_half = pl.ds(pl.multiple_of(c * QH, QH), QH)
    far_half = pl.ds(pl.multiple_of((1 - c) * QH, QH), QH)
    for a in reversed(range(NA)):
        rows = QI * (a + 1)
        tile = pl.ds(offsets[a], 2 * rows)
        gt_s[a] = jnp.zeros((HD, QR), F32)

        def step(k, carry, a=a, rows=rows, tile=tile):
            t = plane_at(k)
            delta = st_s[a, 2:3]
            factor = jnp.exp2((mb_s[t, a : a + 1] - st_s[a, 0:1]) * c2) * st_s[a, 1:2]
            prob = p_s[t, tile] * factor
            ds = (prob * (pg_s[t, tile] - delta)).astype(BF)
            dk = jnp.dot(ds, qa_s[a], preferred_element_type=F32)
            dv = jnp.dot(prob.astype(BF), ga_s[a], preferred_element_type=F32)
            for xd in range(2):
                slot = index(xd, t, c)
                part = slice(xd * rows, (xd + 1) * rows)
                if a == NA - 1:
                    dacc[slot, :rows, :HD] = dk[part]
                    dacc[slot, :rows, HD:] = dv[part]
                else:
                    dacc[slot, :rows, :HD] += dk[part]
                    dacc[slot, :rows, HD:] += dv[part]
            gt_s[a] += t_dot(keys_of(t, rows, slice(0, HD)), ds)
            to_x(a, t)
            if a + 1 < NA:
                to_z(a + 1, k, t)
            return carry

        lax.fori_loop(0, NZ, step, 0)
        gq_mine[a] = gt_s[a, :, far_half]
        remote(gq_mine.at[a], gq_buf.at[a], gsnd.at[a], grcv.at[a], ctx=sib).start()

    def settle(a):
        val = acc[a]
        for d in (1, NZ - 1, 2, NZ - 2, 3, NZ - 3, half_z):
            t = (z + d) % NZ
            take(buf3.at[a, t], r3.at[a, t])
            val = val + buf3[a, t].astype(F32)
        piece = slice(a * QI, (a + 1) * QI)
        gs[mine, piece] = val.astype(BF)
        gkv_ref[piece] = val.astype(BF)
        for peer in (dg, xn, sib):
            ref = gs.at[mine, piece]
            remote(ref, ref, s4, r4.at[mine], ctx=peer).start()

    def queries_done(a):
        take(gq_buf.at[a], grcv.at[a])
        gq = ((gt_s[a, :, own_half] + gq_buf[a]) * SCALE).T.astype(BF)
        for h in range(HEADS):
            gq_ref[a * QI : (a + 1) * QI, h * HD : (h + 1) * HD] = gq[h * QI : (h + 1) * QI]

    settle(3)
    queries_done(3)

    def last(k, carry):
        to_z(0, k, plane_at(k))
        return carry

    lax.fori_loop(0, NZ, last, 0)
    settle(2)
    settle(1)
    queries_done(2)
    queries_done(1)
    queries_done(0)
    settle(0)
    pltpu.make_async_copy(xs.at[mine], xs.at[mine], xown).wait()
    for xd, cd in groups:
        take(xs.at[xd * 2 + cd], xrcv.at[xd * 2 + cd])
    for xd, cd in groups:
        take(gs.at[xd * 2 + cd], r4.at[xd * 2 + cd])
    sends = []
    group = gs[...].reshape(4 * TOK, 2 * HD)
    rows = 2 * HD // DP
    wide = NZ * HD // NW
    for k in range(NW):
        cols = slice(k * wide, (k + 1) * wide)
        wt[:, cols] = lax.dot_general(
            group,
            xs[:, :, cols].reshape(4 * TOK, wide),
            (((0,), (0,)), ((), ())),
            preferred_element_type=F32,
        )
        sw[:, :, cols] = wt[:, cols].astype(BF).reshape(DP, rows, wide)
        for peer in dp_peers:
            copy = remote(
                sw.at[peer, :, cols], buf4.at[dp, :, cols], s5.at[peer, k], r5.at[dp, k], dp=peer
            )
            copy.start()
            sends.append(copy)
    own_rows = pl.ds(pl.multiple_of(dp * rows, rows), rows)
    per = wide // HD
    for k in range(NW):
        cols = slice(k * wide, (k + 1) * wide)
        part = wt[own_rows, cols]
        for peer in dp_peers:
            take(buf4.at[peer, :, cols], r5.at[peer, k])
            part = part + buf4[peer, :, cols].astype(F32)
        for n in range(per):
            t = k * per + n
            wz[t] = part[:, n * HD : (n + 1) * HD]

            @pl.when(z != t)
            def _():
                sb[t] = wz[t].astype(BF)
                remote(sb.at[t], buf5.at[z], s6.at[t], r6.at[z], ctx=index(x, t, c)).start()

    total = wz[z]
    for d in (1, NZ - 1, 2, NZ - 2, 3, NZ - 3, half_z):
        t = (z + d) % NZ
        take(buf5.at[t], r6.at[t])
        total = total + buf5[t].astype(F32)
        sends.append(remote(sb.at[t], buf5.at[z], s6.at[t], r6.at[z], ctx=index(x, t, c)))
    w8[dp] = total * (1.0 / DP)
    for peer in dp_peers:
        copy = remote(w8.at[dp], w8.at[dp], s7.at[peer], r7.at[dp], dp=peer)
        copy.start()
        sends.append(copy)
    for peer in dp_peers:
        take(w8.at[peer], r7.at[peer])
    w_ref[...] = w8[...].reshape(2 * HD, HD).T
    for copy in sends:
        copy.wait_send()

    def sent(ref, sem):
        remote(ref, ref, sem, r1, ctx=sib).wait_send()

    sent(kvall.at[pl.ds(0, 3 + 2 + 10)], snd)
    sent(q2_ref, qsnd.at[0])
    sent(g2_ref, qsnd.at[1])
    for a in range(NA):
        sent(gq_mine.at[a], gsnd.at[a])
    sent(xs.at[pl.ds(0, 3)], xsnd)
    sent(sx, s2)
    sent(sz, s3)
    sent(gs.at[pl.ds(0, 3)], s4)


def write_kernel(a_in, b_in, c_in, a_out, b_out, c_out):
    a_out[...] = a_in[...]
    b_out[...] = b_in[...]
    c_out[...] = c_in[...]


def write(*arrays):
    vmem = pl.BlockSpec(memory_space=pltpu.VMEM)
    return pl.pallas_call(
        write_kernel,
        out_shape=tuple(jax.ShapeDtypeStruct(a.shape, a.dtype) for a in arrays),
        in_specs=[vmem] * 3,
        out_specs=(vmem,) * 3,
        name="write_results",
    )(*arrays)


def on_device(inputs, queries, keys_values, out_grad, lengths):
    vmem = pl.BlockSpec(memory_space=pltpu.VMEM)
    hbm = pl.BlockSpec(memory_space=pl.ANY)
    sem = pltpu.SemaphoreType.DMA
    tri = QI * NA * (NA + 1)
    rows = 2 * HD // DP
    piece = (QI, 2 * HD)
    grad_q, grad_kv, weight = pl.pallas_call(
        fused_kernel,
        out_shape=(
            jax.ShapeDtypeStruct((TOK, HEADS * HD), BF),
            jax.ShapeDtypeStruct((TOK, 2 * HD), BF),
            jax.ShapeDtypeStruct((HD, 2 * HD), F32),
        ),
        in_specs=[pl.BlockSpec(memory_space=pltpu.SMEM), hbm, hbm, hbm, hbm],
        out_specs=(vmem, vmem, vmem),
        scratch_shapes=[
            pltpu.VMEM((TOK, HEADS * HD), BF),
            pltpu.VMEM((TOK, HEADS * HD), BF),
            pltpu.VMEM((TOK, HEADS * HD), BF),
            pltpu.VMEM((TOK, HEADS * HD), BF),
            pltpu.VMEM((STRIPES, TOK, 2 * HD), BF),
            pltpu.VMEM((4, TOK, NZ * HD), BF),
            pltpu.VMEM((NA, QR, HD), BF),
            pltpu.VMEM((NA, QR, HD), BF),
            pltpu.VMEM((2, TOK, HD), jnp.int32),
            pltpu.VMEM((NA, 8, QR), jnp.int32),
            pltpu.VMEM((NA, 8, QR), F32),
            pltpu.VMEM((NA, 8, QR), F32),
            pltpu.VMEM((NZ, 8, QR), F32),
            pltpu.VMEM((NZ, tri, QR), F32),
            pltpu.VMEM((NZ, tri, QR), F32),
            pltpu.VMEM((STRIPES, TOK, 2 * HD), F32),
            pltpu.VMEM((NA, HD, QR), F32),
            pltpu.VMEM((NA, HD, QH), F32),
            pltpu.VMEM((NA, HD, QH), F32),
            pltpu.VMEM((NA, NZ) + piece, BF),
            pltpu.VMEM((NA, NZ) + piece, BF),
            pltpu.VMEM((NA, NZ - 1) + piece, BF),
            pltpu.VMEM((NA, NZ) + piece, BF),
            pltpu.VMEM((NA,) + piece, F32),
            pltpu.VMEM((4, TOK, 2 * HD), BF),
            pltpu.VMEM((2 * HD, NZ * HD), F32),
            pltpu.VMEM((DP, rows, NZ * HD), BF),
            pltpu.VMEM((DP, rows, NZ * HD), BF),
            pltpu.VMEM((NZ, rows, HD), F32),
            pltpu.VMEM((NZ, rows, HD), BF),
            pltpu.VMEM((NZ, rows, HD), BF),
            pltpu.VMEM((DP, rows, HD), F32),
            sem((3,)),
            sem, sem((STRIPES, 2)),
            sem, sem, sem((4,)),
            sem((2,)), sem((2,)),
            sem, sem,
            sem((NA,)), sem((NA,)),
            sem, sem((NA, NZ)),
            sem, sem((NA, NZ)),
            sem, sem((4,)),
            sem((DP, NW)), sem((DP, NW)),
            sem((NZ,)), sem((NZ,)),
            sem((DP,)), sem((DP,)),
        ],
        compiler_params=pltpu.CompilerParams(collective_id=0, has_side_effects=True, vmem_limit_bytes=56 << 20),
        name="fused_backward",
    )(lengths, inputs[0, 0], queries[0, 0], keys_values[0, 0], out_grad[0, 0])
    grad_q, grad_kv, weight = write(grad_q, grad_kv, weight)
    return grad_q[None, None], grad_kv[None, None], weight


def solution(mesh):
    return jax.shard_map(
        on_device,
        mesh=mesh,
        in_specs=(
            P("dp", "ctx", None, None),
            P("dp", "ctx", None, None),
            P("dp", "ctx", None, None),
            P("dp", "ctx", None, None),
            P("dp", None),
        ),
        out_specs=(P("dp", "ctx", None, None), P("dp", "ctx", None, None), P("ctx", None)),
        check_vma=False,
    )
```

```python
import functools
import math

import jax
import jax.numpy as jnp
from jax import lax
from jax.experimental import pallas as pl
from jax.experimental.pallas import tpu as pltpu
from jax.sharding import PartitionSpec as P

HD = 128
HEADS = 8
TOK = 128
STRIPES = 32
NZ = STRIPES // 4
RESPONSES = 4
PIECES = 10
DP = 8
D = 4096
QI = 32
QH = QI * HEADS
QR = 2 * QH
NA = TOK // QI
HT = TOK // 2
NW = 4
SCALE = HD ** -0.5
LOG2E = math.log2(math.e)
NEG = -1e30
MESH = pl.DeviceIdType.MESH
BF = jnp.bfloat16
F32 = jnp.float32


def place():
    ctx = lax.axis_index("ctx")
    return ctx // (2 * NZ), (ctx // 2) % NZ, ctx % 2


def index(x, z, c):
    return x * (2 * NZ) + z * 2 + c


def greet(ctx_peers, dp_peers):
    barrier = pltpu.get_barrier_semaphore()
    for peer in ctx_peers:
        pl.semaphore_signal(barrier, inc=1, device_id={"ctx": peer}, device_id_type=MESH)
    for peer in dp_peers:
        pl.semaphore_signal(barrier, inc=1, device_id={"dp": peer}, device_id_type=MESH)
    pl.semaphore_wait(barrier, len(ctx_peers) + len(dp_peers))


def remote(src, dst, send_sem, recv_sem, **device):
    return pltpu.make_async_remote_copy(
        src_ref=src, dst_ref=dst, send_sem=send_sem, recv_sem=recv_sem, device_id=device, device_id_type=MESH
    )


def dot_t(a, b):
    return lax.dot_general(a, b, (((1,), (1,)), ((), ())), preferred_element_type=F32)


def t_dot(a, b):
    return lax.dot_general(a, b, (((0,), (0,)), ((), ())), preferred_element_type=F32)


def fused_kernel(
    len_ref, x_ref, q_hbm, kv_hbm, g_hbm, gq_ref, gkv_ref, w_ref,
    q_ref, g_ref, q2_ref, g2_ref, kvall, xs, qa_s, ga_s, k0_s, th_s, st_s, st2, mb_s, p_s, pg_s, dacc, gt_s, gq_mine, gq_buf,
    sx, buf2, sz, buf3, acc, gs, wt, sw, buf4, wz, sb, buf5, w8,
    in_sem, snd, rcv, xown, xsnd, xrcv, qsnd, qrcv, s1, r1, gsnd, grcv, s2, r2, s3, r3, s4, r4, s5, r5, s6, r6, s7, r7,
):
    x, z, c = place()
    dp = lax.axis_index("dp")
    me = index(x, z, c)
    mine = x * 2 + c
    sib, xn, dg = index(x, z, 1 - c), index(1 - x, z, c), index(1 - x, z, 1 - c)
    up, dn = index(x, (z + 1) % NZ, c), index(x, (z + NZ - 1) % NZ, c)
    z_peers = [index(x, (z + d) % NZ, c) for d in range(1, NZ)]
    dp_peers = [(dp + d) % DP for d in range(1, DP)]
    own_kv = pltpu.make_async_copy(kv_hbm, kvall.at[me], in_sem.at[0])
    own_q = pltpu.make_async_copy(q_hbm, q_ref, in_sem.at[1])
    own_g = pltpu.make_async_copy(g_hbm, g_ref, in_sem.at[2])
    for copy in (own_kv, own_q, own_g):
        copy.start()
    greet([sib, xn, dg] + z_peers, dp_peers)
    own_kv.wait()

    def send(slot, h, peer):
        ref = kvall.at[slot, pl.ds(h * HT, HT)]
        remote(ref, ref, snd, rcv.at[slot, h], ctx=peer).start()

    def take(ref, recv_sem):
        remote(ref, ref, snd, recv_sem, ctx=sib).wait_recv()

    def arrive(slot, h):
        take(kvall.at[slot, pl.ds(h * HT, HT)], rcv.at[slot, h])

    for h in range(2):
        for peer in (xn, up, dn):
            send(me, h, peer)
    remote(q_hbm, q2_ref, qsnd.at[0], qrcv.at[0], ctx=sib).start()
    remote(g_hbm, g2_ref, qsnd.at[1], qrcv.at[1], ctx=sib).start()
    groups = ((x, 1 - c), (1 - x, c), (1 - x, 1 - c))
    for xd, cd in groups:
        for zd in range(NZ):
            cols = pl.ds(pl.multiple_of(index(xd, zd, cd) * HD, HD), HD)
            dst = xs.at[mine, :, pl.ds(zd * HD, HD)]
            remote(x_ref.at[:, cols], dst, xsnd, xrcv.at[mine], ctx=index(xd, z, cd)).start()
    for zd in range(NZ):
        cols = pl.ds(pl.multiple_of(index(x, zd, c) * HD, HD), HD)
        pltpu.make_async_copy(x_ref.at[:, cols], xs.at[mine, :, pl.ds(zd * HD, HD)], xown).start()

    ends = []
    total_len = jnp.int32(0)
    for k in range(PIECES):
        total_len = total_len + len_ref[0, k]
        ends.append(total_len)
    e0, e4, e5 = ends[0], ends[RESPONSES], ends[RESPONSES + 1]
    shape3 = (2, TOK, HD)
    which = lax.broadcasted_iota(jnp.int32, shape3, 0)
    k0_s[...] = lax.broadcasted_iota(jnp.int32, shape3, 1) * STRIPES + which * (2 * NZ)
    for a in range(NA):
        lane = lax.broadcasted_iota(jnp.int32, (1, QR), 1)
        pos = (a * QI + lane % QI) * STRIPES + index(x, z, 0) + lane // QH
        start = jnp.zeros((1, QR), jnp.int32)
        for e in ends:
            start = jnp.where(pos >= e, e, start)
        th_s[a, 0:1] = pos
        th_s[a, 1:2] = start
        th_s[a, 2:3] = jnp.where(pos < e4, e0, e5)
        th_s[a, 3:4] = jnp.where(pos < e4, 0, e4)
        st_s[a, 0:1] = jnp.full((1, QR), NEG, F32)
        st_s[a, 1:8] = jnp.zeros((7, QR), F32)
    other = index(1 - x, z, c)
    for h in range(2):
        arrive(other, h)
        for peer in (up, dn):
            send(other, h, peer)
    own_q.wait()
    own_g.wait()
    take(q2_ref, qrcv.at[0])
    take(g2_ref, qrcv.at[1])
    for core, q_in, g_in in ((c, q_ref, g_ref), (1 - c, q2_ref, g2_ref)):
        for a in range(NA):
            q_rows = slice(a * QI, (a + 1) * QI)
            for h in range(HEADS):
                to = pl.ds(pl.multiple_of(core * QH + h * QI, QI), QI)
                qa_s[a, to] = q_in[q_rows, h * HD : (h + 1) * HD]
                ga_s[a, to] = g_in[q_rows, h * HD : (h + 1) * HD]
    c2 = SCALE * LOG2E
    offsets = [QI * a * (a + 1) for a in range(NA)]

    def keys_of(t, rows, cols):
        pair = [kvall[pl.ds(index(xd, t, c), 1), :rows, cols] for xd in range(2)]
        return jnp.concatenate(pair, axis=0).reshape(2 * rows, HD)

    def scores_of(n, carry):
        far = (n + 1) // 2
        t = (z + (1 - n % 2) * far + (n % 2) * (NZ - far)) % NZ
        base = 2 * t + c
        for a in range(NA):
            rows = QI * (a + 1)
            s = dot_t(keys_of(t, rows, slice(0, HD)), qa_s[a])
            pg = dot_t(keys_of(t, rows, slice(HD, 2 * HD)), ga_s[a])
            tile = pl.ds(offsets[a], 2 * rows)
            pg_s[t, tile] = pg
            k0 = k0_s[:, :rows].reshape(2 * rows, HD)
            for core in range(2):
                at = slice(core * QH, core * QH + HD)
                mask = (k0 <= th_s[a, 0:1, at] - base) & (
                    (k0 >= th_s[a, 1:2, at] - base)
                    | ((k0 < th_s[a, 2:3, at] - base) & (k0 >= th_s[a, 3:4, at] - base))
                )
                for half in range(QH // HD):
                    cols = slice(core * QH + half * HD, core * QH + (half + 1) * HD)
                    sm = jnp.where(mask, s[:, cols], NEG)
                    m_old = st_s[a, 0:1, cols]
                    m_new = jnp.maximum(m_old, jnp.max(sm, axis=0, keepdims=True))
                    p = jnp.exp2((sm - m_new) * c2)
                    alpha = jnp.exp2((m_old - m_new) * c2)
                    p_s[t, tile, cols] = p
                    st_s[a, 0:1, cols] = m_new
                    st_s[a, 1:2, cols] = st_s[a, 1:2, cols] * alpha + jnp.sum(p, axis=0, keepdims=True)
                    st_s[a, 2:3, cols] = st_s[a, 2:3, cols] * alpha + jnp.sum(p * pg[:, cols], axis=0, keepdims=True)
                    mb_s[t, a : a + 1, cols] = m_new
        return carry

    half_z = NZ // 2

    def travel(d, carry):
        below, above = (z + NZ - d) % NZ, (z + d) % NZ
        for side in range(2):
            for h in range(2):
                for way in range(2):
                    slot = index(x if side == 0 else 1 - x, below if way == 0 else above, c)
                    reach = half_z if way == side else half_z - 1

                    @pl.when((d > 0) & (d <= reach))
                    def _():
                        arrive(slot, h)

                    @pl.when((d > 0) & (d < reach))
                    def _():
                        send(slot, h, up if way == 0 else dn)

        lax.fori_loop(jnp.maximum(2 * d - 1, 0), jnp.minimum(2 * d + 1, NZ), scores_of, 0)
        return carry

    lax.fori_loop(0, half_z + 1, travel, 0)
    remote(st_s, st2, s1, r1, ctx=sib).start()
    take(st2, r1)
    remote(st_s, st_s, s1, r1, ctx=sib).wait_send()
    for a in range(NA):
        m_fin = jnp.maximum(st_s[a, 0:1], st2[a, 0:1])
        low, high = jnp.exp2((st_s[a, 0:1] - m_fin) * c2), jnp.exp2((st2[a, 0:1] - m_fin) * c2)
        inv = 1.0 / (st_s[a, 1:2] * low + st2[a, 1:2] * high)
        delta = (st_s[a, 2:3] * low + st2[a, 2:3] * high) * inv
        st_s[a, 0:1] = m_fin
        st_s[a, 1:2] = inv
        st_s[a, 2:3] = delta

    lane2 = lax.broadcasted_iota(jnp.int32, (1, 2 * HD), 1)
    scale_row = jnp.where(lane2 < HD, SCALE, 1.0).astype(F32)

    def plane_at(k):
        return (z + half_z + (1 - 2 * (k % 2)) * ((k + 1) // 2)) % NZ

    def final_rows(slot, a):
        return dacc[slot, a * QI : (a + 1) * QI] * scale_row

    def to_x(a, t):
        sx[a, t] = final_rows(index(1 - x, t, c), a).astype(BF)
        remote(sx.at[a, t], buf2.at[a, t], s2, r2.at[a, t], ctx=xn).start()

    def to_z(a, k, t):
        take(buf2.at[a, t], r2.at[a, t])
        val = final_rows(index(x, t, c), a) + buf2[a, t].astype(F32)

        @pl.when(k < NZ - 1)
        def _():
            sz[a, k] = val.astype(BF)
            remote(sz.at[a, k], buf3.at[a, z], s3, r3.at[a, z], ctx=index(x, t, c)).start()

        @pl.when(k == NZ - 1)
        def _():
            acc[a] = val

    own_half = pl.ds(pl.multiple_of(c * QH, QH), QH)
    far_half = pl.ds(pl.multiple_of((1 - c) * QH, QH), QH)
    for a in reversed(range(NA)):
        rows = QI * (a + 1)
        tile = pl.ds(offsets[a], 2 * rows)
        gt_s[a] = jnp.zeros((HD, QR), F32)

        def step(k, carry, a=a, rows=rows, tile=tile):
            t = plane_at(k)
            delta = st_s[a, 2:3]
            factor = jnp.exp2((mb_s[t, a : a + 1] - st_s[a, 0:1]) * c2) * st_s[a, 1:2]
            prob = p_s[t, tile] * factor
            ds = (prob * (pg_s[t, tile] - delta)).astype(BF)
            dk = jnp.dot(ds, qa_s[a], preferred_element_type=F32)
            dv = jnp.dot(prob.astype(BF), ga_s[a], preferred_element_type=F32)
            for xd in range(2):
                slot = index(xd, t, c)
                part = slice(xd * rows, (xd + 1) * rows)
                if a == NA - 1:
                    dacc[slot, :rows, :HD] = dk[part]
                    dacc[slot, :rows, HD:] = dv[part]
                else:
                    dacc[slot, :rows, :HD] += dk[part]
                    dacc[slot, :rows, HD:] += dv[part]
            gt_s[a] += t_dot(keys_of(t, rows, slice(0, HD)), ds)
            to_x(a, t)
            if a + 1 < NA:
                to_z(a + 1, k, t)
            return carry

        lax.fori_loop(0, NZ, step, 0)
        gq_mine[a] = gt_s[a, :, far_half]
        remote(gq_mine.at[a], gq_buf.at[a], gsnd.at[a], grcv.at[a], ctx=sib).start()

    def settle(a):
        val = acc[a]
        for d in (1, NZ - 1, 2, NZ - 2, 3, NZ - 3, half_z):
            t = (z + d) % NZ
            take(buf3.at[a, t], r3.at[a, t])
            val = val + buf3[a, t].astype(F32)
        piece = slice(a * QI, (a + 1) * QI)
        gs[mine, piece] = val.astype(BF)
        gkv_ref[piece] = val.astype(BF)
        for peer in (dg, xn, sib):
            ref = gs.at[mine, piece]
            remote(ref, ref, s4, r4.at[mine], ctx=peer).start()

    def queries_done(a):
        take(gq_buf.at[a], grcv.at[a])
        gq = ((gt_s[a, :, own_half] + gq_buf[a]) * SCALE).T.astype(BF)
        for h in range(HEADS):
            gq_ref[a * QI : (a + 1) * QI, h * HD : (h + 1) * HD] = gq[h * QI : (h + 1) * QI]

    settle(3)
    queries_done(3)

    def last(k, carry):
        to_z(0, k, plane_at(k))
        return carry

    lax.fori_loop(0, NZ, last, 0)
    settle(2)
    settle(1)
    queries_done(2)
    queries_done(1)
    queries_done(0)
    settle(0)
    pltpu.make_async_copy(xs.at[mine], xs.at[mine], xown).wait()
    for xd, cd in groups:
        take(xs.at[xd * 2 + cd], xrcv.at[xd * 2 + cd])
    for xd, cd in groups:
        take(gs.at[xd * 2 + cd], r4.at[xd * 2 + cd])
    sends = []
    group = gs[...].reshape(4 * TOK, 2 * HD)
    rows = 2 * HD // DP
    wide = NZ * HD // NW
    for k in range(NW):
        cols = slice(k * wide, (k + 1) * wide)
        wt[:, cols] = lax.dot_general(
            group,
            xs[:, :, cols].reshape(4 * TOK, wide),
            (((0,), (0,)), ((), ())),
            preferred_element_type=F32,
        )
        sw[:, :, cols] = wt[:, cols].astype(BF).reshape(DP, rows, wide)
        for peer in dp_peers:
            copy = remote(
                sw.at[peer, :, cols], buf4.at[dp, :, cols], s5.at[peer, k], r5.at[dp, k], dp=peer
            )
            copy.start()
            sends.append(copy)
    own_rows = pl.ds(pl.multiple_of(dp * rows, rows), rows)
    per = wide // HD
    for k in range(NW):
        cols = slice(k * wide, (k + 1) * wide)
        part = wt[own_rows, cols]
        for peer in dp_peers:
            take(buf4.at[peer, :, cols], r5.at[peer, k])
            part = part + buf4[peer, :, cols].astype(F32)
        for n in range(per):
            t = k * per + n
            wz[t] = part[:, n * HD : (n + 1) * HD]

            @pl.when(z != t)
            def _():
                sb[t] = wz[t].astype(BF)
                remote(sb.at[t], buf5.at[z], s6.at[t], r6.at[z], ctx=index(x, t, c)).start()

    total = wz[z]
    for d in (1, NZ - 1, 2, NZ - 2, 3, NZ - 3, half_z):
        t = (z + d) % NZ
        take(buf5.at[t], r6.at[t])
        total = total + buf5[t].astype(F32)
        sends.append(remote(sb.at[t], buf5.at[z], s6.at[t], r6.at[z], ctx=index(x, t, c)))
    w8[dp] = total * (1.0 / DP)
    for peer in dp_peers:
        copy = remote(w8.at[dp], w8.at[dp], s7.at[peer], r7.at[dp], dp=peer)
        copy.start()
        sends.append(copy)
    for peer in dp_peers:
        take(w8.at[peer], r7.at[peer])
    w_ref[...] = w8[...].reshape(2 * HD, HD).T
    for copy in sends:
        copy.wait_send()

    def sent(ref, sem):
        remote(ref, ref, sem, r1, ctx=sib).wait_send()

    sent(kvall.at[pl.ds(0, 3 + 2 + 10)], snd)
    sent(q2_ref, qsnd.at[0])
    sent(g2_ref, qsnd.at[1])
    for a in range(NA):
        sent(gq_mine.at[a], gsnd.at[a])
    sent(xs.at[pl.ds(0, 3)], xsnd)
    sent(sx, s2)
    sent(sz, s3)
    sent(gs.at[pl.ds(0, 3)], s4)


def write_kernel(a_in, b_in, c_in, a_out, b_out, c_out):
    a_out[...] = a_in[...]
    b_out[...] = b_in[...]
    c_out[...] = c_in[...]


def write(*arrays):
    vmem = pl.BlockSpec(memory_space=pltpu.VMEM)
    return pl.pallas_call(
        write_kernel,
        out_shape=tuple(jax.ShapeDtypeStruct(a.shape, a.dtype) for a in arrays),
        in_specs=[vmem] * 3,
        out_specs=(vmem,) * 3,
        name="write_results",
    )(*arrays)


def on_device(inputs, queries, keys_values, out_grad, lengths):
    vmem = pl.BlockSpec(memory_space=pltpu.VMEM)
    hbm = pl.BlockSpec(memory_space=pltpu.HBM)
    sem = pltpu.SemaphoreType.DMA
    tri = QI * NA * (NA + 1)
    rows = 2 * HD // DP
    piece = (QI, 2 * HD)
    grad_q, grad_kv, weight = pl.pallas_call(
        fused_kernel,
        out_shape=(
            jax.ShapeDtypeStruct((TOK, HEADS * HD), BF),
            jax.ShapeDtypeStruct((TOK, 2 * HD), BF),
            jax.ShapeDtypeStruct((HD, 2 * HD), F32),
        ),
        in_specs=[pl.BlockSpec(memory_space=pltpu.SMEM), hbm, hbm, hbm, hbm],
        out_specs=(vmem, vmem, vmem),
        scratch_shapes=[
            pltpu.VMEM((TOK, HEADS * HD), BF),
            pltpu.VMEM((TOK, HEADS * HD), BF),
            pltpu.VMEM((TOK, HEADS * HD), BF),
            pltpu.VMEM((TOK, HEADS * HD), BF),
            pltpu.VMEM((STRIPES, TOK, 2 * HD), BF),
            pltpu.VMEM((4, TOK, NZ * HD), BF),
            pltpu.VMEM((NA, QR, HD), BF),
            pltpu.VMEM((NA, QR, HD), BF),
            pltpu.VMEM((2, TOK, HD), jnp.int32),
            pltpu.VMEM((NA, 8, QR), jnp.int32),
            pltpu.VMEM((NA, 8, QR), F32),
            pltpu.VMEM((NA, 8, QR), F32),
            pltpu.VMEM((NZ, 8, QR), F32),
            pltpu.VMEM((NZ, tri, QR), F32),
            pltpu.VMEM((NZ, tri, QR), F32),
            pltpu.VMEM((STRIPES, TOK, 2 * HD), F32),
            pltpu.VMEM((NA, HD, QR), F32),
            pltpu.VMEM((NA, HD, QH), F32),
            pltpu.VMEM((NA, HD, QH), F32),
            pltpu.VMEM((NA, NZ) + piece, BF),
            pltpu.VMEM((NA, NZ) + piece, BF),
            pltpu.VMEM((NA, NZ - 1) + piece, BF),
            pltpu.VMEM((NA, NZ) + piece, BF),
            pltpu.VMEM((NA,) + piece, F32),
            pltpu.VMEM((4, TOK, 2 * HD), BF),
            pltpu.VMEM((2 * HD, NZ * HD), F32),
            pltpu.VMEM((DP, rows, NZ * HD), BF),
            pltpu.VMEM((DP, rows, NZ * HD), BF),
            pltpu.VMEM((NZ, rows, HD), F32),
            pltpu.VMEM((NZ, rows, HD), BF),
            pltpu.VMEM((NZ, rows, HD), BF),
            pltpu.VMEM((DP, rows, HD), F32),
            sem((3,)),
            sem, sem((STRIPES, 2)),
            sem, sem, sem((4,)),
            sem((2,)), sem((2,)),
            sem, sem,
            sem((NA,)), sem((NA,)),
            sem, sem((NA, NZ)),
            sem, sem((NA, NZ)),
            sem, sem((4,)),
            sem((DP, NW)), sem((DP, NW)),
            sem((NZ,)), sem((NZ,)),
            sem((DP,)), sem((DP,)),
        ],
        compiler_params=pltpu.CompilerParams(collective_id=0, has_side_effects=True, vmem_limit_bytes=48 << 20),
        name="fused_backward",
    )(pltpu.with_memory_space_constraint(lengths, pltpu.HBM), *(pltpu.with_memory_space_constraint(a[0, 0], pltpu.HBM) for a in (inputs, queries, keys_values, out_grad)))
    held = [pltpu.with_memory_space_constraint(a, pltpu.VMEM) for a in (grad_q, grad_kv, weight)]
    grad_q, grad_kv, weight = write(*held)
    return grad_q[None, None], grad_kv[None, None], weight


def solution(mesh):
    return jax.shard_map(
        on_device,
        mesh=mesh,
        in_specs=(
            P("dp", "ctx", None, None),
            P("dp", "ctx", None, None),
            P("dp", "ctx", None, None),
            P("dp", "ctx", None, None),
            P("dp", None),
        ),
        out_specs=(P("dp", "ctx", None, None), P("dp", "ctx", None, None), P("ctx", None)),
        check_vma=False,
    )
```
